32 devices in a mesh: slab: 4 (over y, x), dom: 8 (over z, core).
Axes of the slice: x: 2, y: 2, z: 4, core: 2. Of those that a mesh axis runs over, the one named last changes fastest.
Arguments:
- tiles: bfloat16 [2560, 128, 128], P('dom'), may hold values from -0.09375 to 0.09375
- volume: float32 [256, 128, 128], P(('slab', 'dom')), parts along dimension 0, may hold values from 0 to 2
- tile_voxel: int32 [2560], P('dom'), may hold values from 0 to 7
- tile_dest: int32 [2560], P('dom'), may hold values from 0 to 7
- slot_block: int32 [8, 8], P('dom'), may hold values from 0 to 7
- tile_count: int32 [8], P('dom'), may hold values from 80 to 320, as said below
- counts: int32 [256, 128, 128], P(('slab', 'dom')), parts along dimension 0, may hold values from 2000 to 29999
Outputs:
- updated: float32 [256, 128, 128], P(('slab', 'dom')), parts along dimension 0
- residual: bfloat16 [256, 128, 128], P(('slab', 'dom')), parts along dimension 0
The draws below stay inside these ranges and needn't reach their ends.
There are 4 independent parts, one for each index of `slab`. The reference program is written for one: setup_inputs(seed, part) draws one part's arguments, and reference() takes and returns one part's arrays. A program takes and returns all parts, laid end to end along the dimension named above; an argument that names none is the same for every part. Nothing has to cross between parts.
Inputs may be any that keep to these rules, and one draw needn't show every extreme that they name: `tile_count`: every device holds at least max(80, 3) live tiles; some device holds 320.
All inputs are finite; a program needn't handle non-finite values.
Results may differ from the reference program's by a relative error of at most 0.006.
Values may be sent and summed in bfloat16 or wider, within the bound.
A program may use at most 128 MiB of HBM per device.

```python
import jax
import jax.numpy as jnp
from jax import lax

TILE = 128
SLICES = 128
TPD = 320
VBD = 8
RBD = 8
VOXBLK = 64
RAYBLK = 64
ALLTILES = 2560
N_DOM = 8


def draw_tile_count(key, part):
    first, second = jax.random.split(jax.random.fold_in(key, 11))
    lowest = max(TPD // 4, 3)
    base = jax.random.randint(first, (N_DOM,), lowest, max(TPD // 2, lowest) + 1)
    busiest = jax.random.randint(second, (), 0, N_DOM)
    return jnp.where(jnp.arange(N_DOM) == busiest, TPD, base).astype(jnp.int32)


def draw_tile_dest(key, part):
    source = jax.random.fold_in(key, 23)
    base = jax.random.randint(source, (N_DOM, TPD), 0, N_DOM)
    holder = jnp.arange(N_DOM, dtype=jnp.int32)
    base = base.at[:, 0].set((holder + 1) % N_DOM)
    base = base.at[:, 1].set((holder + N_DOM // 2) % N_DOM)
    base = base.at[:, 2].set((holder + N_DOM - 1) % N_DOM)
    return base.reshape(N_DOM * TPD).astype(jnp.int32)


def with_ends(result, own_key, smallest, largest):
    shape = result.shape
    index_at = [jax.random.randint(jax.random.fold_in(own_key, axis), (), 0, shape[axis]) for axis in range(len(shape))]
    result = result.at[tuple(index_at)].set(smallest)
    longest = shape.index(max(shape))
    index_at[longest] = (index_at[longest] + 1) % shape[longest]
    return result.at[tuple(index_at)].set(largest)


def steps_of(rng, extent, shards, smallest, top_value):
    gain = 1.0
    for dim, parts in shards:
        steps = jax.random.uniform(jax.random.fold_in(jax.random.fold_in(rng, 6), dim), (parts,), jnp.float32, smallest / len(shards), top_value / len(shards))
        gain = gain * jnp.repeat(jnp.exp(steps), extent[dim] // parts).reshape((-1,) + (1,) * (len(extent) - 1 - dim))
    return gain


def bell_draw(key, shape, width, bound, pieces=(), held_as=jnp.bfloat16):
    array = jax.random.normal(key, shape, jnp.float32) * width
    if len(pieces) > 0:
        array = steps_of(key, shape, pieces, -0.22, 0.18) * array
    return jnp.clip(array, min=-bound, max=bound).astype(held_as)


def setup_inputs(seed: int = 0, part: int = 0) -> dict:
    seeds = jax.random.split(jax.random.key(seed), 8)
    part_splits = jax.random.split(jax.random.fold_in(seeds[7], part), 8)
    tiles = bell_draw(seeds[0], (ALLTILES, TILE, TILE), (TILE * 32) ** -0.5, 0.09375, ((0, 8),))
    volume = jnp.clip(2.0 * jax.random.uniform(part_splits[1], (VOXBLK, TILE, SLICES), jnp.float32) ** steps_of(part_splits[1], (VOXBLK, TILE, SLICES), ((0, 8),), -0.2, 0.2), 0.0, 2.0)
    tile_voxel = with_ends(jax.random.randint(seeds[2], (ALLTILES,), 0, VBD), jax.random.fold_in(seeds[2], 1), 0, VBD - 1).astype(jnp.int32)
    tile_dest = draw_tile_dest(jax.random.fold_in(seeds[7], 71), part)
    slot_block = with_ends(jax.random.randint(seeds[4], (N_DOM, N_DOM), 0, RBD), jax.random.fold_in(seeds[4], 1), 0, RBD - 1).astype(jnp.int32)
    tile_count = draw_tile_count(jax.random.fold_in(seeds[7], 71), part)
    counts = with_ends(jax.random.randint(part_splits[6], (RAYBLK, TILE, SLICES), 2000, 30000), jax.random.fold_in(part_splits[6], 1), 2000, 29999).astype(jnp.int32)
    return dict(tiles=tiles, volume=volume, tile_voxel=tile_voxel, tile_dest=tile_dest, slot_block=slot_block, tile_count=tile_count, counts=counts)


flux = 32768.0
step_size = 0.5


def reference(tiles, volume, tile_voxel, tile_dest, slot_block, tile_count, counts):
    voxels_low = volume.astype(jnp.bfloat16)
    slots = jnp.arange(N_DOM * TPD, dtype=jnp.int32)
    holder = (slots // TPD).astype(jnp.int32)
    alive_mask = ((slots % TPD) < tile_count[holder]).astype(jnp.float32)
    ray_block = (tile_dest * RBD + slot_block[tile_dest, holder]).astype(jnp.int32)
    voxel_index = (holder * VBD + tile_voxel).astype(jnp.int32)
    tile_groups = tiles.reshape(N_DOM, TPD, TILE, TILE)
    inputs = (tile_groups, voxel_index.reshape(N_DOM, TPD), ray_block.reshape(N_DOM, TPD), alive_mask.reshape(N_DOM, TPD))

    def forward(running, item):
        group, voxels, blocks, alive = item
        picked = voxels_low[voxels].astype(jnp.float32)
        products = jnp.einsum('tab,tbs->tas', group.astype(jnp.float32), picked)
        products = products * alive[:, None, None]
        return running + jax.ops.segment_sum(products, blocks, num_segments=RAYBLK), None

    sinogram, _ = lax.scan(forward, jnp.zeros((RAYBLK, TILE, SLICES), jnp.float32), inputs)
    measured = jnp.log(flux / counts.astype(jnp.float32))
    residual = (sinogram - measured).astype(jnp.bfloat16)

    def backward(running, item):
        group, voxels, blocks, alive = item
        fetched = residual[blocks].astype(jnp.float32)
        products = jnp.einsum('tab,tas->tbs', group.astype(jnp.float32), fetched)
        products = products * alive[:, None, None]
        return running + jax.ops.segment_sum(products, voxels, num_segments=VOXBLK), None

    gradient, _ = lax.scan(backward, jnp.zeros((VOXBLK, TILE, SLICES), jnp.float32), inputs)
    updated = jnp.maximum(volume - step_size * gradient, 0.0)
    return updated, residual
```

```python
import functools

import jax
import jax.numpy as jnp
from jax import lax
from jax.experimental import pallas as pl
from jax.experimental.pallas import tpu as pltpu
from jax.sharding import PartitionSpec as P

flux = 32768.0
step_size = 0.5
GROUP = 16
PARTS = 4
PHASES = 2
VMEM_BUDGET = 40 * 1024 * 1024


def fold_kernel(voxel_blocks, dest_ref, voxel_ref, count_ref, tiles_ref, w_ref, tile_buf, sems, *acc):
    slots, rows, cols = tile_buf.shape
    groups = slots // GROUP
    part = rows // PARTS
    count = count_ref[0]

    def fetch(g):
        at = pl.ds(g * GROUP, GROUP)
        return pltpu.make_async_copy(tiles_ref.at[at], tile_buf.at[at], sems.at[g])

    for g in range(groups):
        @pl.when(g * GROUP < count)
        def _(g=g):
            fetch(g).start()

    for a in acc:
        a[...] = jnp.zeros_like(a)

    def add_tile(i):
        bucket = dest_ref[i] * voxel_blocks + voxel_ref[i]
        for q, a in enumerate(acc):
            a[bucket] += tile_buf[i, q * part:(q + 1) * part, :].astype(jnp.float32)

    @pl.loop(0, groups)
    def _(g):
        live = jnp.clip(count - g * GROUP, 0, GROUP)

        @pl.when(live > 0)
        def _():
            fetch(g).wait()

        @pl.when(live == GROUP)
        def _():
            for j in range(GROUP):
                add_tile(g * GROUP + j)

        @pl.when(live < GROUP)
        def _():
            @pl.loop(0, live)
            def _(j):
                add_tile(g * GROUP + j)

    peers = w_ref.shape[0] // rows

    @pl.loop(0, peers)
    def _(d):
        for v in range(voxel_blocks):
            for q, a in enumerate(acc):
                w_ref[pl.ds(pl.multiple_of(d * rows + q * part, part), part), v * cols:(v + 1) * cols] = (
                    a[d * voxel_blocks + v].astype(jnp.bfloat16))


def peer_order(n, me):
    chips = n // 2
    z, core = me // 2, me % 2
    sign = 1 - 2 * (z % 2)
    hops = sorted(range(1, chips), key=lambda k: (abs(2 * k - chips), k))
    order = []
    for k in hops:
        there = (z - sign * k + chips) % chips
        order += [there * 2 + core, there * 2 + 1 - core]
    return order + [z * 2 + 1 - core]


def exchange_kernel(n, slot_ref, w_ref, volume_ref, counts_ref, updated_ref, residual_ref,
                    out_buf, in_buf, answer_buf, back_buf, low, measured, grad,
                    out_send, out_recv, back_send, back_recv):
    me = lax.axis_index("dom")
    blocks, rows, lanes = volume_ref.shape
    owned = counts_ref.shape[0]
    step = rows // PHASES
    order = peer_order(n, me)

    barrier = pltpu.get_barrier_semaphore()
    for peer in order:
        pl.semaphore_signal(barrier, inc=1, device_id={"dom": peer}, device_id_type=pl.DeviceIdType.MESH)

    for v in range(blocks):
        low[v * rows:(v + 1) * rows, :] = volume_ref[v].astype(jnp.bfloat16)

    def project(d, p):
        at = pl.ds(pl.multiple_of(d * rows + p * step, step), step)
        return jnp.dot(w_ref[at, :], low[...], preferred_element_type=jnp.float32).astype(jnp.bfloat16)

    def send(src, dst, send_sems, recv_sems, peer, p):
        return pltpu.make_async_remote_copy(
            src_ref=src.at[peer, p], dst_ref=dst.at[me, p],
            send_sem=send_sems.at[peer, p], recv_sem=recv_sems.at[me, p],
            device_id={"dom": peer}, device_id_type=pl.DeviceIdType.MESH)

    def arrival(dst, send_sems, recv_sems, peer, p):
        return pltpu.make_async_remote_copy(
            src_ref=dst.at[peer, p], dst_ref=dst.at[peer, p],
            send_sem=send_sems.at[peer, p], recv_sem=recv_sems.at[peer, p],
            device_id={"dom": peer}, device_id_type=pl.DeviceIdType.MESH)

    first = True
    for p in range(PHASES):
        for peer in order:
            out_buf[peer, p] = project(peer, p)
            if first:
                pl.semaphore_wait(barrier, n - 1)
                first = False
            send(out_buf, in_buf, out_send, out_recv, peer, p).start()
    for p in range(PHASES):
        in_buf[me, p] = project(me, p)
    for b in range(owned):
        measured[b] = jnp.log(flux / counts_ref[b].astype(jnp.float32))

    for p in range(PHASES):
        for peer in reversed(order):
            arrival(in_buf, out_send, out_recv, peer, p).wait_recv()
        at = slice(p * step, (p + 1) * step)
        for b in range(owned):
            total = jnp.zeros((step, lanes), jnp.float32)
            for s in range(n):
                total += jnp.where(slot_ref[0, s] == b, in_buf[s, p].astype(jnp.float32), 0.0)
            residual_ref[b, at, :] = (total - measured[b, at, :]).astype(jnp.bfloat16)
        for peer in order:
            answer_buf[peer, p] = residual_ref[slot_ref[0, peer], at, :]
            send(answer_buf, back_buf, back_send, back_recv, peer, p).start()
        back_buf[me, p] = residual_ref[slot_ref[0, me], at, :]

    def pull(d):
        held = back_buf[d].reshape(rows, lanes)
        at = pl.ds(pl.multiple_of(d * rows, rows), rows)
        return jnp.dot(held.T, w_ref[at, :], preferred_element_type=jnp.float32)

    grad[...] = pull(me)
    for peer in reversed(order):
        for p in range(PHASES):
            arrival(back_buf, back_send, back_recv, peer, p).wait_recv()
        grad[...] += pull(peer)
    for v in range(blocks):
        updated_ref[v] = jnp.maximum(
            volume_ref[v] - step_size * grad[:, v * rows:(v + 1) * rows].T, 0.0)
    for p in range(PHASES):
        for peer in order:
            send(out_buf, in_buf, out_send, out_recv, peer, p).wait_send()
            send(answer_buf, back_buf, back_send, back_recv, peer, p).wait_send()


def fused(tiles, volume, tile_voxel, tile_dest, slot_block, tile_count, counts):
    n = lax.axis_size("dom")
    slots, rows, cols = tiles.shape
    blocks, _, lanes = volume.shape
    smem = pl.BlockSpec(memory_space=pltpu.SMEM)
    vmem = pl.BlockSpec(memory_space=pltpu.VMEM)
    anywhere = pl.BlockSpec(memory_space=pl.ANY)
    weights = pl.pallas_call(
        functools.partial(fold_kernel, blocks),
        out_shape=jax.ShapeDtypeStruct((n * rows, blocks * cols), jnp.bfloat16),
        in_specs=[smem, smem, smem, anywhere],
        out_specs=vmem,
        scratch_shapes=[
            pltpu.VMEM(tiles.shape, tiles.dtype),
            pltpu.SemaphoreType.DMA((slots // GROUP,)),
        ] + [pltpu.VMEM((n * blocks, rows // PARTS, cols), jnp.float32)] * PARTS,
        name="fold_tiles",
    )(tile_dest, tile_voxel, tile_count, tiles)

    split = (n, PHASES, rows // PHASES, lanes)
    updated, residual = pl.pallas_call(
        functools.partial(exchange_kernel, n),
        out_shape=(
            jax.ShapeDtypeStruct(volume.shape, jnp.float32),
            jax.ShapeDtypeStruct(counts.shape, jnp.bfloat16),
        ),
        in_specs=[smem, vmem, vmem, vmem],
        out_specs=(vmem, vmem),
        scratch_shapes=[pltpu.VMEM(split, jnp.bfloat16)] * 4 + [
            pltpu.VMEM((blocks * rows, lanes), jnp.bfloat16),
            pltpu.VMEM(counts.shape, jnp.float32),
            pltpu.VMEM((lanes, blocks * rows), jnp.float32),
        ] + [pltpu.SemaphoreType.DMA((n, PHASES))] * 4,
        compiler_params=pltpu.CompilerParams(collective_id=0, has_side_effects=True),
        name="exchange",
    )(slot_block, weights, volume, counts)
    return updated, residual


def general(tiles, volume, tile_voxel, tile_dest, slot_block, tile_count, counts):
    peer_count = lax.axis_size("dom")
    tile_slots, tile_rows = tiles.shape[:2]
    voxel_blocks, _, slice_count = volume.shape
    alive = jnp.arange(tile_slots, dtype=jnp.int32) < tile_count[0]
    picked = volume.astype(jnp.bfloat16)[tile_voxel]
    products = jnp.einsum("tab,tbs->tas", tiles, picked, preferred_element_type=jnp.float32)
    outgoing = (
        jnp.zeros((peer_count, tile_rows, slice_count), jnp.float32)
        .at[jnp.where(alive, tile_dest, peer_count)]
        .add(products, mode="drop")
    )
    incoming = lax.all_to_all(
        outgoing.astype(jnp.bfloat16), "dom", split_axis=0, concat_axis=0, tiled=True
    ).astype(jnp.float32)
    sinogram = jnp.zeros(counts.shape, jnp.float32).at[slot_block[0]].add(incoming)
    measured = jnp.log(flux / counts.astype(jnp.float32))
    residual = (sinogram - measured).astype(jnp.bfloat16)
    returned = lax.all_to_all(residual[slot_block[0]], "dom", split_axis=0, concat_axis=0, tiled=True)
    back = jnp.einsum("tab,tas->tbs", tiles, returned[tile_dest], preferred_element_type=jnp.float32)
    gradient = (
        jnp.zeros(volume.shape, jnp.float32)
        .at[jnp.where(alive, tile_voxel, voxel_blocks)]
        .add(back, mode="drop")
    )
    return jnp.maximum(volume - step_size * gradient, 0.0), residual


def on_device(tiles, volume, *rest):
    n = lax.axis_size("dom")
    need = tiles.size * 2 + n * volume.shape[0] * tiles.shape[1] * tiles.shape[2] * 6
    if need > VMEM_BUDGET or n % 2 or tiles.shape[0] % GROUP:
        return general(tiles, volume, *rest)
    return fused(tiles, volume, *rest)


def solution(mesh):
    both = P(("slab", "dom"), None, None)
    in_specs = (P("dom", None, None), both, P("dom"), P("dom"), P("dom", None), P("dom"), both)
    return jax.shard_map(on_device, mesh=mesh, in_specs=in_specs, out_specs=(both, both), check_vma=False)
```

```python
import functools

import jax
import jax.numpy as jnp
from jax import lax
from jax.experimental import pallas as pl
from jax.experimental.pallas import tpu as pltpu
from jax.sharding import PartitionSpec as P

flux = 32768.0
step_size = 0.5
GROUP = 16
PARTS = 4
PHASES = 2
FOLD_VMEM = 57 * 1024 * 1024
EXCHANGE_VMEM = 10 * 1024 * 1024
VMEM_BUDGET = 18 * 1024 * 1024


def fold_kernel(voxel_blocks, dest_hbm, voxel_hbm, count_hbm, tiles_ref, w_ref,
                dest_ref, voxel_ref, count_ref, tile_buf, table_sems, sems, *acc):
    slots, rows, cols = tile_buf.shape
    groups = slots // GROUP
    part = rows // PARTS
    tables = [
        pltpu.make_async_copy(src, dst, table_sems.at[i])
        for i, (src, dst) in enumerate(
            ((dest_hbm, dest_ref), (voxel_hbm, voxel_ref), (count_hbm, count_ref)))
    ]
    for table in tables:
        table.start()

    def fetch(g):
        at = pl.ds(g * GROUP, GROUP)
        return pltpu.make_async_copy(tiles_ref.at[at], tile_buf.at[at], sems.at[g])

    for g in range(groups):
        fetch(g).start()

    for a in acc:
        a[...] = jnp.zeros_like(a)
    for table in tables:
        table.wait()
    count = count_ref[0]

    def add_tile(i):
        bucket = dest_ref[i] * voxel_blocks + voxel_ref[i]
        for q, a in enumerate(acc):
            a[bucket] += tile_buf[i, q * part:(q + 1) * part, :].astype(jnp.float32)

    @pl.loop(0, groups)
    def _(g):
        live = jnp.clip(count - g * GROUP, 0, GROUP)

        fetch(g).wait()

        @pl.when(live == GROUP)
        def _():
            for j in range(GROUP):
                add_tile(g * GROUP + j)

        @pl.when(live < GROUP)
        def _():
            @pl.loop(0, live)
            def _(j):
                add_tile(g * GROUP + j)

    peers = w_ref.shape[0] // rows

    @pl.loop(0, peers)
    def _(d):
        for v in range(voxel_blocks):
            for q, a in enumerate(acc):
                w_ref[pl.ds(pl.multiple_of(d * rows + q * part, part), part), v * cols:(v + 1) * cols] = (
                    a[d * voxel_blocks + v].astype(jnp.bfloat16))


def peer_order(n, me):
    chips = n // 2
    z, core = me // 2, me % 2
    sign = 1 - 2 * (z % 2)
    hops = sorted(range(1, chips), key=lambda k: (abs(2 * k - chips), k))
    order = []
    for k in hops:
        there = (z - sign * k + chips) % chips
        order += [there * 2 + core, there * 2 + 1 - core]
    return order + [z * 2 + 1 - core]


def exchange_kernel(n, slot_ref, w_ref, volume_ref, counts_ref, updated_ref, residual_ref,
                    out_buf, in_buf, answer_buf, back_buf, low, measured, grad,
                    out_send, out_recv, back_send, back_recv):
    me = lax.axis_index("dom")
    blocks, rows, lanes = volume_ref.shape
    owned = counts_ref.shape[0]
    step = rows // PHASES
    order = peer_order(n, me)

    barrier = pltpu.get_barrier_semaphore()
    for peer in order:
        pl.semaphore_signal(barrier, inc=1, device_id={"dom": peer}, device_id_type=pl.DeviceIdType.MESH)

    for v in range(blocks):
        low[v * rows:(v + 1) * rows, :] = volume_ref[v].astype(jnp.bfloat16)

    def project(d, p):
        at = pl.ds(pl.multiple_of(d * rows + p * step, step), step)
        return jnp.dot(w_ref[at, :], low[...], preferred_element_type=jnp.float32).astype(jnp.bfloat16)

    def send(src, dst, send_sems, recv_sems, peer, p):
        return pltpu.make_async_remote_copy(
            src_ref=src.at[peer, p], dst_ref=dst.at[me, p],
            send_sem=send_sems.at[peer, p], recv_sem=recv_sems.at[me, p],
            device_id={"dom": peer}, device_id_type=pl.DeviceIdType.MESH)

    def arrival(dst, send_sems, recv_sems, peer, p):
        return pltpu.make_async_remote_copy(
            src_ref=dst.at[peer, p], dst_ref=dst.at[peer, p],
            send_sem=send_sems.at[peer, p], recv_sem=recv_sems.at[peer, p],
            device_id={"dom": peer}, device_id_type=pl.DeviceIdType.MESH)

    first = True
    for p in range(PHASES):
        for peer in order:
            out_buf[peer, p] = project(peer, p)
            if first:
                pl.semaphore_wait(barrier, n - 1)
                first = False
            send(out_buf, in_buf, out_send, out_recv, peer, p).start()
    for p in range(PHASES):
        in_buf[me, p] = project(me, p)
    for b in range(owned):
        measured[b] = jnp.log(flux / counts_ref[b].astype(jnp.float32))

    for p in range(PHASES):
        for peer in reversed(order):
            arrival(in_buf, out_send, out_recv, peer, p).wait_recv()
        at = slice(p * step, (p + 1) * step)
        for b in range(owned):
            total = jnp.zeros((step, lanes), jnp.float32)
            for s in range(n):
                total += jnp.where(slot_ref[0, s] == b, in_buf[s, p].astype(jnp.float32), 0.0)
            residual_ref[b, at, :] = (total - measured[b, at, :]).astype(jnp.bfloat16)
        for peer in order:
            answer_buf[peer, p] = residual_ref[slot_ref[0, peer], at, :]
            send(answer_buf, back_buf, back_send, back_recv, peer, p).start()
        back_buf[me, p] = residual_ref[slot_ref[0, me], at, :]

    def pull(d):
        held = back_buf[d].reshape(rows, lanes)
        at = pl.ds(pl.multiple_of(d * rows, rows), rows)
        return jnp.dot(held.T, w_ref[at, :], preferred_element_type=jnp.float32)

    grad[...] = pull(me)
    for peer in reversed(order):
        for p in range(PHASES):
            arrival(back_buf, back_send, back_recv, peer, p).wait_recv()
        grad[...] += pull(peer)
    for v in range(blocks):
        updated_ref[v] = jnp.maximum(
            volume_ref[v] - step_size * grad[:, v * rows:(v + 1) * rows].T, 0.0)
    for p in range(PHASES):
        for peer in order:
            send(out_buf, in_buf, out_send, out_recv, peer, p).wait_send()
            send(answer_buf, back_buf, back_send, back_recv, peer, p).wait_send()


def fused(tiles, volume, tile_voxel, tile_dest, slot_block, tile_count, counts):
    n = lax.axis_size("dom")
    slots, rows, cols = tiles.shape
    blocks, _, lanes = volume.shape
    smem = pl.BlockSpec(memory_space=pltpu.SMEM)
    vmem = pl.BlockSpec(memory_space=pltpu.VMEM)
    hbm = pl.BlockSpec(memory_space=pltpu.HBM)
    weights = pl.pallas_call(
        functools.partial(fold_kernel, blocks),
        out_shape=pltpu.VMEM((n * rows, blocks * cols), jnp.bfloat16),
        in_specs=[hbm] * 4,
        out_specs=vmem,
        scratch_shapes=[
            pltpu.SMEM(tile_dest.shape, jnp.int32),
            pltpu.SMEM(tile_voxel.shape, jnp.int32),
            pltpu.SMEM(tile_count.shape, jnp.int32),
            pltpu.VMEM(tiles.shape, tiles.dtype),
            pltpu.SemaphoreType.DMA((3,)),
            pltpu.SemaphoreType.DMA((slots // GROUP,)),
        ] + [pltpu.VMEM((n * blocks, rows // PARTS, cols), jnp.float32)] * PARTS,
        compiler_params=pltpu.CompilerParams(vmem_limit_bytes=FOLD_VMEM),
        name="fold_tiles",
    )(tile_dest, tile_voxel, tile_count, tiles)

    split = (n, PHASES, rows // PHASES, lanes)
    updated, residual = pl.pallas_call(
        functools.partial(exchange_kernel, n),
        out_shape=(
            jax.ShapeDtypeStruct(volume.shape, jnp.float32),
            jax.ShapeDtypeStruct(counts.shape, jnp.bfloat16),
        ),
        in_specs=[smem, vmem, vmem, vmem],
        out_specs=(vmem, vmem),
        scratch_shapes=[pltpu.VMEM(split, jnp.bfloat16)] * 4 + [
            pltpu.VMEM((blocks * rows, lanes), jnp.bfloat16),
            pltpu.VMEM(counts.shape, jnp.float32),
            pltpu.VMEM((lanes, blocks * rows), jnp.float32),
        ] + [pltpu.SemaphoreType.DMA((n, PHASES))] * 4,
        compiler_params=pltpu.CompilerParams(collective_id=0, has_side_effects=True, vmem_limit_bytes=EXCHANGE_VMEM),
        name="exchange",
    )(slot_block, weights, volume, counts)
    return updated, residual


def general(tiles, volume, tile_voxel, tile_dest, slot_block, tile_count, counts):
    peer_count = lax.axis_size("dom")
    tile_slots, tile_rows = tiles.shape[:2]
    voxel_blocks, _, slice_count = volume.shape
    alive = jnp.arange(tile_slots, dtype=jnp.int32) < tile_count[0]
    picked = volume.astype(jnp.bfloat16)[tile_voxel]
    products = jnp.einsum("tab,tbs->tas", tiles, picked, preferred_element_type=jnp.float32)
    outgoing = (
        jnp.zeros((peer_count, tile_rows, slice_count), jnp.float32)
        .at[jnp.where(alive, tile_dest, peer_count)]
        .add(products, mode="drop")
    )
    incoming = lax.all_to_all(
        outgoing.astype(jnp.bfloat16), "dom", split_axis=0, concat_axis=0, tiled=True
    ).astype(jnp.float32)
    sinogram = jnp.zeros(counts.shape, jnp.float32).at[slot_block[0]].add(incoming)
    measured = jnp.log(flux / counts.astype(jnp.float32))
    residual = (sinogram - measured).astype(jnp.bfloat16)
    returned = lax.all_to_all(residual[slot_block[0]], "dom", split_axis=0, concat_axis=0, tiled=True)
    back = jnp.einsum("tab,tas->tbs", tiles, returned[tile_dest], preferred_element_type=jnp.float32)
    gradient = (
        jnp.zeros(volume.shape, jnp.float32)
        .at[jnp.where(alive, tile_voxel, voxel_blocks)]
        .add(back, mode="drop")
    )
    return jnp.maximum(volume - step_size * gradient, 0.0), residual


def on_device(tiles, volume, *rest):
    n = lax.axis_size("dom")
    need = tiles.size * 2 + n * volume.shape[0] * tiles.shape[1] * tiles.shape[2] * 6
    if need > VMEM_BUDGET or n % 2 or tiles.shape[0] % GROUP:
        return general(tiles, volume, *rest)
    return fused(tiles, volume, *rest)


def solution(mesh):
    both = P(("slab", "dom"), None, None)
    in_specs = (P("dom", None, None), both, P("dom"), P("dom"), P("dom", None), P("dom"), both)
    return jax.shard_map(on_device, mesh=mesh, in_specs=in_specs, out_specs=(both, both), check_vma=False)
```

```python
import functools

import jax
import jax.numpy as jnp
from jax import lax
from jax.experimental import pallas as pl
from jax.experimental.pallas import tpu as pltpu
from jax.sharding import PartitionSpec as P

flux = 32768.0
step_size = 0.5
GROUP = 16
PARTS = 4
PHASES = 2
FOLD_VMEM = 53 * 1024 * 1024
EXCHANGE_VMEM = 10 * 1024 * 1024
VMEM_BUDGET = 18 * 1024 * 1024


def fold_kernel(voxel_blocks, dest_hbm, voxel_hbm, count_hbm, tiles_ref, *refs):
    acc, (dest_ref, voxel_ref, count_ref, tile_buf, table_sems, sems) = refs[:PARTS], refs[PARTS:]
    slots, rows, cols = tile_buf.shape
    groups = slots // GROUP
    part = rows // PARTS
    tables = [
        pltpu.make_async_copy(src, dst, table_sems.at[i])
        for i, (src, dst) in enumerate(
            ((dest_hbm, dest_ref), (voxel_hbm, voxel_ref), (count_hbm, count_ref)))
    ]
    for table in tables:
        table.start()

    def fetch(g):
        at = pl.ds(g * GROUP, GROUP)
        return pltpu.make_async_copy(tiles_ref.at[at], tile_buf.at[at], sems.at[g])

    for g in range(groups):
        fetch(g).start()

    for a in acc:
        a[...] = jnp.zeros_like(a)
    for table in tables:
        table.wait()
    count = count_ref[0]

    def add_tile(i):
        bucket = dest_ref[i] * voxel_blocks + voxel_ref[i]
        for q, a in enumerate(acc):
            a[bucket] += tile_buf[i, q * part:(q + 1) * part, :].astype(jnp.float32)

    @pl.loop(0, groups)
    def _(g):
        live = jnp.clip(count - g * GROUP, 0, GROUP)

        fetch(g).wait()

        @pl.when(live == GROUP)
        def _():
            for j in range(GROUP):
                add_tile(g * GROUP + j)

        @pl.when(live < GROUP)
        def _():
            @pl.loop(0, live)
            def _(j):
                add_tile(g * GROUP + j)


def peer_order(n, me):
    chips = n // 2
    z, core = me // 2, me % 2
    sign = 1 - 2 * (z % 2)
    hops = sorted(range(1, chips), key=lambda k: (abs(2 * k - chips), k))
    order = []
    for k in hops:
        there = (z - sign * k + chips) % chips
        order += [there * 2 + core, there * 2 + 1 - core]
    return order + [z * 2 + 1 - core]


def exchange_kernel(n, slot_ref, volume_ref, counts_ref, *refs):
    acc, (grad_ref, residual_ref), scratch = refs[:PARTS], refs[PARTS:PARTS + 2], refs[PARTS + 2:]
    (out_buf, in_buf, answer_buf, landing, w_ref, low, measured,
     out_send, out_recv, back_send, back_recv) = scratch
    me = lax.axis_index("dom")
    blocks, rows, lanes = volume_ref.shape
    owned = counts_ref.shape[0]
    step = rows // PHASES
    part = rows // PARTS
    order = peer_order(n, me)

    barrier = pltpu.get_barrier_semaphore()
    for peer in order:
        pl.semaphore_signal(barrier, inc=1, device_id={"dom": peer}, device_id_type=pl.DeviceIdType.MESH)

    for v in range(blocks):
        low[v * rows:(v + 1) * rows, :] = volume_ref[v].astype(jnp.bfloat16)

    def project(d, p):
        for q in range(p * step // part, (p + 1) * step // part):
            at = pl.ds(pl.multiple_of(d * rows + q * part, part), part)
            for v in range(blocks):
                w_ref[at, v * rows:(v + 1) * rows] = acc[q][d * blocks + v].astype(jnp.bfloat16)
        at = pl.ds(pl.multiple_of(d * rows + p * step, step), step)
        return jnp.dot(w_ref[at, :], low[...], preferred_element_type=jnp.float32).astype(jnp.bfloat16)

    def send(src, dst, send_sems, recv_sems, peer, p):
        return pltpu.make_async_remote_copy(
            src_ref=src.at[peer, p], dst_ref=dst.at[me, p],
            send_sem=send_sems.at[peer, p], recv_sem=recv_sems.at[me, p],
            device_id={"dom": peer}, device_id_type=pl.DeviceIdType.MESH)

    def arrival(dst, send_sems, recv_sems, peer, p):
        return pltpu.make_async_remote_copy(
            src_ref=dst.at[peer, p], dst_ref=dst.at[peer, p],
            send_sem=send_sems.at[peer, p], recv_sem=recv_sems.at[peer, p],
            device_id={"dom": peer}, device_id_type=pl.DeviceIdType.MESH)

    first = True
    for p in range(PHASES):
        for peer in order:
            out_buf[peer, p] = project(peer, p)
            if first:
                pl.semaphore_wait(barrier, n - 1)
                first = False
            send(out_buf, in_buf, out_send, out_recv, peer, p).start()
    for p in range(PHASES):
        in_buf[me, p] = project(me, p)
    for b in range(owned):
        measured[b] = jnp.log(flux / counts_ref[b].astype(jnp.float32))

    for p in range(PHASES):
        for peer in reversed(order):
            arrival(in_buf, out_send, out_recv, peer, p).wait_recv()
        at = slice(p * step, (p + 1) * step)
        for b in range(owned):
            total = jnp.zeros((step, lanes), jnp.float32)
            for s in range(n):
                total += jnp.where(slot_ref[0, s] == b, in_buf[s, p].astype(jnp.float32), 0.0)
            residual_ref[b, at, :] = (total - measured[b, at, :]).astype(jnp.bfloat16)
        for peer in order:
            answer_buf[peer, p] = residual_ref[slot_ref[0, peer], at, :]
            send(answer_buf, landing, back_send, back_recv, peer, p).start()
        landing[me, p] = residual_ref[slot_ref[0, me], at, :]

    def pull(d):
        held = landing[d].reshape(rows, lanes)
        at = pl.ds(pl.multiple_of(d * rows, rows), rows)
        return jnp.dot(held.T, w_ref[at, :], preferred_element_type=jnp.float32)

    grad_ref[...] = pull(me)
    for peer in reversed(order):
        for p in range(PHASES):
            arrival(landing, back_send, back_recv, peer, p).wait_recv()
        grad_ref[...] += pull(peer)
    for p in range(PHASES):
        for peer in order:
            send(out_buf, in_buf, out_send, out_recv, peer, p).wait_send()
            send(answer_buf, landing, back_send, back_recv, peer, p).wait_send()


def finish_kernel(volume_ref, grad_ref, residual_ref, updated_hbm, residual_hbm, updated, sems):
    blocks, rows, _ = volume_ref.shape
    copies = [pltpu.make_async_copy(residual_ref, residual_hbm, sems.at[blocks])]
    copies[0].start()
    for v in range(blocks):
        updated[v] = jnp.maximum(
            volume_ref[v] - step_size * grad_ref[:, v * rows:(v + 1) * rows].T, 0.0)
        copies.append(pltpu.make_async_copy(updated.at[v], updated_hbm.at[v], sems.at[v]))
        copies[-1].start()
    for copy in copies:
        copy.wait()


def fused(tiles, volume, tile_voxel, tile_dest, slot_block, tile_count, counts):
    n = lax.axis_size("dom")
    slots, rows, cols = tiles.shape
    blocks, _, lanes = volume.shape
    smem = pl.BlockSpec(memory_space=pltpu.SMEM)
    vmem = pl.BlockSpec(memory_space=pltpu.VMEM)
    hbm = pl.BlockSpec(memory_space=pltpu.HBM)
    sums = pl.pallas_call(
        functools.partial(fold_kernel, blocks),
        out_shape=[pltpu.VMEM((n * blocks, rows // PARTS, cols), jnp.float32)] * PARTS,
        in_specs=[hbm] * 4,
        out_specs=[vmem] * PARTS,
        scratch_shapes=[
            pltpu.SMEM(tile_dest.shape, jnp.int32),
            pltpu.SMEM(tile_voxel.shape, jnp.int32),
            pltpu.SMEM(tile_count.shape, jnp.int32),
            pltpu.VMEM(tiles.shape, tiles.dtype),
            pltpu.SemaphoreType.DMA((3,)),
            pltpu.SemaphoreType.DMA((slots // GROUP,)),
        ],
        compiler_params=pltpu.CompilerParams(vmem_limit_bytes=FOLD_VMEM),
        name="fold_tiles",
    )(tile_dest, tile_voxel, tile_count, tiles)

    split = (n, PHASES, rows // PHASES, lanes)
    gradient, residual = pl.pallas_call(
        functools.partial(exchange_kernel, n),
        out_shape=(
            pltpu.VMEM((lanes, blocks * cols), jnp.float32),
            pltpu.VMEM(counts.shape, jnp.bfloat16),
        ),
        in_specs=[smem] + [vmem] * (2 + PARTS),
        out_specs=(vmem, vmem),
        scratch_shapes=[pltpu.VMEM(split, jnp.bfloat16)] * 4 + [
            pltpu.VMEM((n * rows, blocks * cols), jnp.bfloat16),
            pltpu.VMEM((blocks * cols, lanes), jnp.bfloat16),
            pltpu.VMEM(counts.shape, jnp.float32),
        ] + [pltpu.SemaphoreType.DMA((n, PHASES))] * 4,
        compiler_params=pltpu.CompilerParams(
            collective_id=0, has_side_effects=True, vmem_limit_bytes=EXCHANGE_VMEM),
        name="exchange",
    )(slot_block, volume, counts, *sums)
    return pl.pallas_call(
        finish_kernel,
        out_shape=(
            jax.ShapeDtypeStruct(volume.shape, jnp.float32),
            jax.ShapeDtypeStruct(counts.shape, jnp.bfloat16),
        ),
        in_specs=[vmem, vmem, vmem],
        out_specs=(hbm, hbm),
        scratch_shapes=[
            pltpu.VMEM(volume.shape, jnp.float32),
            pltpu.SemaphoreType.DMA((blocks + 1,)),
        ],
        compiler_params=pltpu.CompilerParams(vmem_limit_bytes=EXCHANGE_VMEM),
        name="finish",
    )(volume, gradient, residual)


def general(tiles, volume, tile_voxel, tile_dest, slot_block, tile_count, counts):
    peer_count = lax.axis_size("dom")
    tile_slots, tile_rows = tiles.shape[:2]
    voxel_blocks, _, slice_count = volume.shape
    alive = jnp.arange(tile_slots, dtype=jnp.int32) < tile_count[0]
    picked = volume.astype(jnp.bfloat16)[tile_voxel]
    products = jnp.einsum("tab,tbs->tas", tiles, picked, preferred_element_type=jnp.float32)
    outgoing = (
        jnp.zeros((peer_count, tile_rows, slice_count), jnp.float32)
        .at[jnp.where(alive, tile_dest, peer_count)]
        .add(products, mode="drop")
    )
    incoming = lax.all_to_all(
        outgoing.astype(jnp.bfloat16), "dom", split_axis=0, concat_axis=0, tiled=True
    ).astype(jnp.float32)
    sinogram = jnp.zeros(counts.shape, jnp.float32).at[slot_block[0]].add(incoming)
    measured = jnp.log(flux / counts.astype(jnp.float32))
    residual = (sinogram - measured).astype(jnp.bfloat16)
    returned = lax.all_to_all(residual[slot_block[0]], "dom", split_axis=0, concat_axis=0, tiled=True)
    back = jnp.einsum("tab,tas->tbs", tiles, returned[tile_dest], preferred_element_type=jnp.float32)
    gradient = (
        jnp.zeros(volume.shape, jnp.float32)
        .at[jnp.where(alive, tile_voxel, voxel_blocks)]
        .add(back, mode="drop")
    )
    return jnp.maximum(volume - step_size * gradient, 0.0), residual


def on_device(tiles, volume, *rest):
    n = lax.axis_size("dom")
    need = tiles.size * 2 + n * volume.shape[0] * tiles.shape[1] * tiles.shape[2] * 6
    if need > VMEM_BUDGET or n % 2 or tiles.shape[0] % GROUP:
        return general(tiles, volume, *rest)
    return fused(tiles, volume, *rest)


def solution(mesh):
    both = P(("slab", "dom"), None, None)
    in_specs = (P("dom", None, None), both, P("dom"), P("dom"), P("dom", None), P("dom"), both)
    return jax.shard_map(on_device, mesh=mesh, in_specs=in_specs, out_specs=(both, both), check_vma=False)
```

```python
import functools

import jax
import jax.numpy as jnp
from jax import lax
from jax.experimental import pallas as pl
from jax.experimental.pallas import tpu as pltpu
from jax.sharding import PartitionSpec as P

flux = 32768.0
step_size = 0.5
GROUP = 16
PARTS = 4
PHASES = 2
FOLD_VMEM = 53 * 1024 * 1024
EXCHANGE_VMEM = 10 * 1024 * 1024
VMEM_BUDGET = 18 * 1024 * 1024


def fold_kernel(voxel_blocks, dest_hbm, voxel_hbm, count_hbm, tiles_ref, *refs):
    acc, (dest_ref, voxel_ref, count_ref, tile_buf, table_sems, sems) = refs[:PARTS], refs[PARTS:]
    slots, rows, cols = tile_buf.shape
    groups = slots // GROUP
    part = rows // PARTS
    tables = [
        pltpu.make_async_copy(src, dst, table_sems.at[i])
        for i, (src, dst) in enumerate(
            ((dest_hbm, dest_ref), (voxel_hbm, voxel_ref), (count_hbm, count_ref)))
    ]
    for table in tables:
        table.start()

    def fetch(g):
        at = pl.ds(g * GROUP, GROUP)
        return pltpu.make_async_copy(tiles_ref.at[at], tile_buf.at[at], sems.at[g])

    for g in range(groups):
        fetch(g).start()

    for a in acc:
        a[...] = jnp.zeros_like(a)
    for table in tables:
        table.wait()
    count = count_ref[0]

    def add_tile(i):
        bucket = dest_ref[i] * voxel_blocks + voxel_ref[i]
        for q, a in enumerate(acc):
            a[bucket] += tile_buf[i, q * part:(q + 1) * part, :].astype(jnp.float32)

    @pl.loop(0, groups)
    def _(g):
        live = jnp.clip(count - g * GROUP, 0, GROUP)

        fetch(g).wait()

        @pl.when(live == GROUP)
        def _():
            for j in range(GROUP):
                add_tile(g * GROUP + j)

        @pl.when(live < GROUP)
        def _():
            @pl.loop(0, live)
            def _(j):
                add_tile(g * GROUP + j)


def peer_order(n, me):
    chips = n // 2
    z, core = me // 2, me % 2
    sign = 1 - 2 * (z % 2)
    hops = sorted(range(1, chips), key=lambda k: (abs(2 * k - chips), k))
    order = []
    for k in hops:
        there = (z - sign * k + chips) % chips
        order += [there * 2 + core, there * 2 + 1 - core]
    return order + [z * 2 + 1 - core]


def exchange_kernel(n, slot_ref, volume_ref, counts_ref, *refs):
    acc, (grad_ref, residual_ref), scratch = refs[:PARTS], refs[PARTS:PARTS + 2], refs[PARTS + 2:]
    (out_buf, in_buf, answer_buf, landing, w_ref, low, measured,
     out_send, out_recv, back_send, back_recv) = scratch
    me = lax.axis_index("dom")
    blocks, rows, lanes = volume_ref.shape
    owned = counts_ref.shape[0]
    step = rows // PHASES
    part = rows // PARTS
    order = peer_order(n, me)

    barrier = pltpu.get_barrier_semaphore()
    for peer in order:
        pl.semaphore_signal(barrier, inc=1, device_id={"dom": peer}, device_id_type=pl.DeviceIdType.MESH)

    for v in range(blocks):
        low[v * rows:(v + 1) * rows, :] = volume_ref[v].astype(jnp.bfloat16)

    def project(d, p):
        at = pl.ds(pl.multiple_of((p * n + d) * step, step), step)
        for q in range(p * step // part, (p + 1) * step // part):
            here = pl.ds(pl.multiple_of((p * n + d) * step + q * part - p * step, part), part)
            for v in range(blocks):
                w_ref[here, v * rows:(v + 1) * rows] = acc[q][d * blocks + v].astype(jnp.bfloat16)
        return jnp.dot(w_ref[at, :], low[...], preferred_element_type=jnp.float32).astype(jnp.bfloat16)

    def send(src, dst, send_sems, recv_sems, peer, p):
        return pltpu.make_async_remote_copy(
            src_ref=src.at[p, peer], dst_ref=dst.at[p, me],
            send_sem=send_sems.at[peer, p], recv_sem=recv_sems.at[me, p],
            device_id={"dom": peer}, device_id_type=pl.DeviceIdType.MESH)

    def arrival(dst, send_sems, recv_sems, peer, p):
        return pltpu.make_async_remote_copy(
            src_ref=dst.at[p, peer], dst_ref=dst.at[p, peer],
            send_sem=send_sems.at[peer, p], recv_sem=recv_sems.at[peer, p],
            device_id={"dom": peer}, device_id_type=pl.DeviceIdType.MESH)

    first = True
    for p in range(PHASES):
        for peer in order:
            out_buf[p, peer] = project(peer, p)
            if first:
                pl.semaphore_wait(barrier, n - 1)
                first = False
            send(out_buf, in_buf, out_send, out_recv, peer, p).start()
    for p in range(PHASES):
        in_buf[p, me] = project(me, p)
    for b in range(owned):
        measured[b] = jnp.log(flux / counts_ref[b].astype(jnp.float32))

    for p in range(PHASES):
        for peer in reversed(order):
            arrival(in_buf, out_send, out_recv, peer, p).wait_recv()
        at = slice(p * step, (p + 1) * step)
        for b in range(owned):
            total = jnp.zeros((step, lanes), jnp.float32)
            for s in range(n):
                total += jnp.where(slot_ref[0, s] == b, in_buf[p, s].astype(jnp.float32), 0.0)
            residual_ref[b, at, :] = (total - measured[b, at, :]).astype(jnp.bfloat16)
        for peer in order:
            answer_buf[p, peer] = residual_ref[slot_ref[0, peer], at, :]
            send(answer_buf, landing, back_send, back_recv, peer, p).start()
        landing[p, me] = residual_ref[slot_ref[0, me], at, :]

    half = n // 2
    near = me // half
    mine = [near * half + (me + j) % half for j in range(1, half)]
    theirs = [(1 - near) * half + j for j in range(half)]

    def pull(p, side):
        start = pl.multiple_of(side * half, half)
        held = landing[p, pl.ds(start, half)].reshape(half * step, lanes)
        at = pl.ds(pl.multiple_of((p * n + start) * step, half * step), half * step)
        return jnp.dot(held.T, w_ref[at, :], preferred_element_type=jnp.float32)

    for p in range(PHASES):
        for side, peers in ((near, mine), (1 - near, theirs)):
            for peer in peers:
                arrival(landing, back_send, back_recv, peer, p).wait_recv()
            if p == 0 and peers is mine:
                grad_ref[...] = pull(p, side)
            else:
                grad_ref[...] += pull(p, side)
    for p in range(PHASES):
        for peer in order:
            send(out_buf, in_buf, out_send, out_recv, peer, p).wait_send()
            send(answer_buf, landing, back_send, back_recv, peer, p).wait_send()


def finish_kernel(volume_ref, grad_ref, residual_ref, updated_hbm, residual_hbm, updated, sems):
    blocks, rows, _ = volume_ref.shape
    copies = [pltpu.make_async_copy(residual_ref, residual_hbm, sems.at[blocks])]
    copies[0].start()
    for v in range(blocks):
        updated[v] = jnp.maximum(
            volume_ref[v] - step_size * grad_ref[:, v * rows:(v + 1) * rows].T, 0.0)
        copies.append(pltpu.make_async_copy(updated.at[v], updated_hbm.at[v], sems.at[v]))
        copies[-1].start()
    for copy in copies:
        copy.wait()


def fused(tiles, volume, tile_voxel, tile_dest, slot_block, tile_count, counts):
    n = lax.axis_size("dom")
    slots, rows, cols = tiles.shape
    blocks, _, lanes = volume.shape
    smem = pl.BlockSpec(memory_space=pltpu.SMEM)
    vmem = pl.BlockSpec(memory_space=pltpu.VMEM)
    hbm = pl.BlockSpec(memory_space=pltpu.HBM)
    sums = pl.pallas_call(
        functools.partial(fold_kernel, blocks),
        out_shape=[pltpu.VMEM((n * blocks, rows // PARTS, cols), jnp.float32)] * PARTS,
        in_specs=[hbm] * 4,
        out_specs=[vmem] * PARTS,
        scratch_shapes=[
            pltpu.SMEM(tile_dest.shape, jnp.int32),
            pltpu.SMEM(tile_voxel.shape, jnp.int32),
            pltpu.SMEM(tile_count.shape, jnp.int32),
            pltpu.VMEM(tiles.shape, tiles.dtype),
            pltpu.SemaphoreType.DMA((3,)),
            pltpu.SemaphoreType.DMA((slots // GROUP,)),
        ],
        compiler_params=pltpu.CompilerParams(vmem_limit_bytes=FOLD_VMEM),
        name="fold_tiles",
    )(tile_dest, tile_voxel, tile_count, tiles)

    split = (PHASES, n, rows // PHASES, lanes)
    gradient, residual = pl.pallas_call(
        functools.partial(exchange_kernel, n),
        out_shape=(
            pltpu.VMEM((lanes, blocks * cols), jnp.float32),
            pltpu.VMEM(counts.shape, jnp.bfloat16),
        ),
        in_specs=[smem] + [vmem] * (2 + PARTS),
        out_specs=(vmem, vmem),
        scratch_shapes=[pltpu.VMEM(split, jnp.bfloat16)] * 4 + [
            pltpu.VMEM((n * rows, blocks * cols), jnp.bfloat16),
            pltpu.VMEM((blocks * cols, lanes), jnp.bfloat16),
            pltpu.VMEM(counts.shape, jnp.float32),
        ] + [pltpu.SemaphoreType.DMA((n, PHASES))] * 4,
        compiler_params=pltpu.CompilerParams(
            collective_id=0, has_side_effects=True, vmem_limit_bytes=EXCHANGE_VMEM),
        name="exchange",
    )(slot_block, volume, counts, *sums)
    return pl.pallas_call(
        finish_kernel,
        out_shape=(
            jax.ShapeDtypeStruct(volume.shape, jnp.float32),
            jax.ShapeDtypeStruct(counts.shape, jnp.bfloat16),
        ),
        in_specs=[vmem, vmem, vmem],
        out_specs=(hbm, hbm),
        scratch_shapes=[
            pltpu.VMEM(volume.shape, jnp.float32),
            pltpu.SemaphoreType.DMA((blocks + 1,)),
        ],
        compiler_params=pltpu.CompilerParams(vmem_limit_bytes=EXCHANGE_VMEM),
        name="finish",
    )(volume, gradient, residual)


def general(tiles, volume, tile_voxel, tile_dest, slot_block, tile_count, counts):
    peer_count = lax.axis_size("dom")
    tile_slots, tile_rows = tiles.shape[:2]
    voxel_blocks, _, slice_count = volume.shape
    alive = jnp.arange(tile_slots, dtype=jnp.int32) < tile_count[0]
    picked = volume.astype(jnp.bfloat16)[tile_voxel]
    products = jnp.einsum("tab,tbs->tas", tiles, picked, preferred_element_type=jnp.float32)
    outgoing = (
        jnp.zeros((peer_count, tile_rows, slice_count), jnp.float32)
        .at[jnp.where(alive, tile_dest, peer_count)]
        .add(products, mode="drop")
    )
    incoming = lax.all_to_all(
        outgoing.astype(jnp.bfloat16), "dom", split_axis=0, concat_axis=0, tiled=True
    ).astype(jnp.float32)
    sinogram = jnp.zeros(counts.shape, jnp.float32).at[slot_block[0]].add(incoming)
    measured = jnp.log(flux / counts.astype(jnp.float32))
    residual = (sinogram - measured).astype(jnp.bfloat16)
    returned = lax.all_to_all(residual[slot_block[0]], "dom", split_axis=0, concat_axis=0, tiled=True)
    back = jnp.einsum("tab,tas->tbs", tiles, returned[tile_dest], preferred_element_type=jnp.float32)
    gradient = (
        jnp.zeros(volume.shape, jnp.float32)
        .at[jnp.where(alive, tile_voxel, voxel_blocks)]
        .add(back, mode="drop")
    )
    return jnp.maximum(volume - step_size * gradient, 0.0), residual


def on_device(tiles, volume, *rest):
    n = lax.axis_size("dom")
    need = tiles.size * 2 + n * volume.shape[0] * tiles.shape[1] * tiles.shape[2] * 6
    if need > VMEM_BUDGET or n % 2 or tiles.shape[0] % GROUP:
        return general(tiles, volume, *rest)
    return fused(tiles, volume, *rest)


def solution(mesh):
    both = P(("slab", "dom"), None, None)
    in_specs = (P("dom", None, None), both, P("dom"), P("dom"), P("dom", None), P("dom"), both)
    return jax.shard_map(on_device, mesh=mesh, in_specs=in_specs, out_specs=(both, both), check_vma=False)
```

```python
import functools

import jax
import jax.numpy as jnp
from jax import lax
from jax.experimental import pallas as pl
from jax.experimental.pallas import tpu as pltpu
from jax.sharding import PartitionSpec as P

flux = 32768.0
step_size = 0.5
GROUP = 32
PARTS = 4
PHASES = 2
FOLD_VMEM = 53 * 1024 * 1024
EXCHANGE_VMEM = 10 * 1024 * 1024
VMEM_BUDGET = 18 * 1024 * 1024


def fold_kernel(voxel_blocks, dest_hbm, voxel_hbm, count_hbm, tiles_ref, *refs):
    acc, (dest_ref, voxel_ref, count_ref, tile_buf, table_sems, sems) = refs[:PARTS], refs[PARTS:]
    slots, rows, cols = tile_buf.shape
    groups = slots // GROUP
    part = rows // PARTS
    tables = [
        pltpu.make_async_copy(src, dst, table_sems.at[i])
        for i, (src, dst) in enumerate(
            ((dest_hbm, dest_ref), (voxel_hbm, voxel_ref), (count_hbm, count_ref)))
    ]
    for table in tables:
        table.start()

    def fetch(g):
        at = pl.ds(g * GROUP, GROUP)
        return pltpu.make_async_copy(tiles_ref.at[at], tile_buf.at[at], sems.at[g])

    for g in range(groups):
        fetch(g).start()

    for a in acc:
        a[...] = jnp.zeros_like(a)
    for table in tables:
        table.wait()
    count = count_ref[0]

    def add_tile(i):
        bucket = dest_ref[i] * voxel_blocks + voxel_ref[i]
        for q, a in enumerate(acc):
            a[bucket] += tile_buf[i, q * part:(q + 1) * part, :].astype(jnp.float32)

    @pl.loop(0, groups)
    def _(g):
        live = jnp.clip(count - g * GROUP, 0, GROUP)

        fetch(g).wait()

        @pl.when(live == GROUP)
        def _():
            for j in range(GROUP):
                add_tile(g * GROUP + j)

        @pl.when(live < GROUP)
        def _():
            @pl.loop(0, live)
            def _(j):
                add_tile(g * GROUP + j)


def peer_order(n, me):
    chips = n // 2
    z, core = me // 2, me % 2
    sign = 1 - 2 * (z % 2)
    hops = sorted(range(1, chips), key=lambda k: (abs(2 * k - chips), k))
    order = []
    for k in hops:
        there = (z - sign * k + chips) % chips
        order += [there * 2 + core, there * 2 + 1 - core]
    return order + [z * 2 + 1 - core]


def exchange_kernel(n, slot_ref, volume_ref, counts_ref, *refs):
    acc, (grad_ref, residual_ref), scratch = refs[:PARTS], refs[PARTS:PARTS + 2], refs[PARTS + 2:]
    (out_buf, in_buf, answer_buf, landing, w_ref, low, measured,
     out_send, out_recv, back_send, back_recv) = scratch
    me = lax.axis_index("dom")
    blocks, rows, lanes = volume_ref.shape
    owned = counts_ref.shape[0]
    step = rows // PHASES
    part = rows // PARTS
    order = peer_order(n, me)

    barrier = pltpu.get_barrier_semaphore()
    for peer in order:
        pl.semaphore_signal(barrier, inc=1, device_id={"dom": peer}, device_id_type=pl.DeviceIdType.MESH)

    for v in range(blocks):
        low[v * rows:(v + 1) * rows, :] = volume_ref[v].astype(jnp.bfloat16)

    def project(d, p):
        at = pl.ds(pl.multiple_of((p * n + d) * step, step), step)
        for q in range(p * step // part, (p + 1) * step // part):
            here = pl.ds(pl.multiple_of((p * n + d) * step + q * part - p * step, part), part)
            for v in range(blocks):
                w_ref[here, v * rows:(v + 1) * rows] = acc[q][d * blocks + v].astype(jnp.bfloat16)
        return jnp.dot(w_ref[at, :], low[...], preferred_element_type=jnp.float32).astype(jnp.bfloat16)

    def send(src, dst, send_sems, recv_sems, peer, p):
        return pltpu.make_async_remote_copy(
            src_ref=src.at[p, peer], dst_ref=dst.at[p, me],
            send_sem=send_sems.at[peer, p], recv_sem=recv_sems.at[me, p],
            device_id={"dom": peer}, device_id_type=pl.DeviceIdType.MESH)

    def arrival(dst, send_sems, recv_sems, peer, p):
        return pltpu.make_async_remote_copy(
            src_ref=dst.at[p, peer], dst_ref=dst.at[p, peer],
            send_sem=send_sems.at[peer, p], recv_sem=recv_sems.at[peer, p],
            device_id={"dom": peer}, device_id_type=pl.DeviceIdType.MESH)

    first = True
    for p in range(PHASES):
        for peer in order:
            out_buf[p, peer] = project(peer, p)
            if first:
                pl.semaphore_wait(barrier, n - 1)
                first = False
            send(out_buf, in_buf, out_send, out_recv, peer, p).start()
    for p in range(PHASES):
        in_buf[p, me] = project(me, p)
    for b in range(owned):
        measured[b] = jnp.log(flux / counts_ref[b].astype(jnp.float32))

    for p in range(PHASES):
        for peer in reversed(order):
            arrival(in_buf, out_send, out_recv, peer, p).wait_recv()
        at = slice(p * step, (p + 1) * step)
        for b in range(owned):
            total = jnp.zeros((step, lanes), jnp.float32)
            for s in range(n):
                total += jnp.where(slot_ref[0, s] == b, in_buf[p, s].astype(jnp.float32), 0.0)
            residual_ref[b, at, :] = (total - measured[b, at, :]).astype(jnp.bfloat16)
        for peer in order:
            answer_buf[p, peer] = residual_ref[slot_ref[0, peer], at, :]
            send(answer_buf, landing, back_send, back_recv, peer, p).start()
        landing[p, me] = residual_ref[slot_ref[0, me], at, :]

    half = n // 2
    near = me // half
    mine = [near * half + (me + j) % half for j in range(1, half)]
    theirs = [(1 - near) * half + j for j in range(half)]

    def pull(p, side):
        start = pl.multiple_of(side * half, half)
        held = landing[p, pl.ds(start, half)].reshape(half * step, lanes)
        at = pl.ds(pl.multiple_of((p * n + start) * step, half * step), half * step)
        return jnp.dot(held.T, w_ref[at, :], preferred_element_type=jnp.float32)

    for p in range(PHASES):
        for side, peers in ((near, mine), (1 - near, theirs)):
            for peer in peers:
                arrival(landing, back_send, back_recv, peer, p).wait_recv()
            if p == 0 and peers is mine:
                grad_ref[...] = pull(p, side)
            else:
                grad_ref[...] += pull(p, side)
    for p in range(PHASES):
        for peer in order:
            send(out_buf, in_buf, out_send, out_recv, peer, p).wait_send()
            send(answer_buf, landing, back_send, back_recv, peer, p).wait_send()


def finish_kernel(volume_ref, grad_ref, residual_ref, updated_hbm, residual_hbm, updated, sems):
    blocks, rows, _ = volume_ref.shape
    copies = [pltpu.make_async_copy(residual_ref, residual_hbm, sems.at[blocks])]
    copies[0].start()
    for v in range(blocks):
        updated[v] = jnp.maximum(
            volume_ref[v] - step_size * grad_ref[:, v * rows:(v + 1) * rows].T, 0.0)
        copies.append(pltpu.make_async_copy(updated.at[v], updated_hbm.at[v], sems.at[v]))
        copies[-1].start()
    for copy in copies:
        copy.wait()


def fused(tiles, volume, tile_voxel, tile_dest, slot_block, tile_count, counts):
    n = lax.axis_size("dom")
    slots, rows, cols = tiles.shape
    blocks, _, lanes = volume.shape
    smem = pl.BlockSpec(memory_space=pltpu.SMEM)
    vmem = pl.BlockSpec(memory_space=pltpu.VMEM)
    hbm = pl.BlockSpec(memory_space=pltpu.HBM)
    sums = pl.pallas_call(
        functools.partial(fold_kernel, blocks),
        out_shape=[pltpu.VMEM((n * blocks, rows // PARTS, cols), jnp.float32)] * PARTS,
        in_specs=[hbm] * 4,
        out_specs=[vmem] * PARTS,
        scratch_shapes=[
            pltpu.SMEM(tile_dest.shape, jnp.int32),
            pltpu.SMEM(tile_voxel.shape, jnp.int32),
            pltpu.SMEM(tile_count.shape, jnp.int32),
            pltpu.VMEM(tiles.shape, tiles.dtype),
            pltpu.SemaphoreType.DMA((3,)),
            pltpu.SemaphoreType.DMA((slots // GROUP,)),
        ],
        compiler_params=pltpu.CompilerParams(vmem_limit_bytes=FOLD_VMEM),
        name="fold_tiles",
    )(tile_dest, tile_voxel, tile_count, tiles)

    split = (PHASES, n, rows // PHASES, lanes)
    gradient, residual = pl.pallas_call(
        functools.partial(exchange_kernel, n),
        out_shape=(
            pltpu.VMEM((lanes, blocks * cols), jnp.float32),
            pltpu.VMEM(counts.shape, jnp.bfloat16),
        ),
        in_specs=[smem] + [vmem] * (2 + PARTS),
        out_specs=(vmem, vmem),
        scratch_shapes=[pltpu.VMEM(split, jnp.bfloat16)] * 4 + [
            pltpu.VMEM((n * rows, blocks * cols), jnp.bfloat16),
            pltpu.VMEM((blocks * cols, lanes), jnp.bfloat16),
            pltpu.VMEM(counts.shape, jnp.float32),
        ] + [pltpu.SemaphoreType.DMA((n, PHASES))] * 4,
        compiler_params=pltpu.CompilerParams(
            collective_id=0, has_side_effects=True, vmem_limit_bytes=EXCHANGE_VMEM),
        name="exchange",
    )(slot_block, volume, counts, *sums)
    return pl.pallas_call(
        finish_kernel,
        out_shape=(
            jax.ShapeDtypeStruct(volume.shape, jnp.float32),
            jax.ShapeDtypeStruct(counts.shape, jnp.bfloat16),
        ),
        in_specs=[vmem, vmem, vmem],
        out_specs=(hbm, hbm),
        scratch_shapes=[
            pltpu.VMEM(volume.shape, jnp.float32),
            pltpu.SemaphoreType.DMA((blocks + 1,)),
        ],
        compiler_params=pltpu.CompilerParams(vmem_limit_bytes=EXCHANGE_VMEM),
        name="finish",
    )(volume, gradient, residual)


def general(tiles, volume, tile_voxel, tile_dest, slot_block, tile_count, counts):
    peer_count = lax.axis_size("dom")
    tile_slots, tile_rows = tiles.shape[:2]
    voxel_blocks, _, slice_count = volume.shape
    alive = jnp.arange(tile_slots, dtype=jnp.int32) < tile_count[0]
    picked = volume.astype(jnp.bfloat16)[tile_voxel]
    products = jnp.einsum("tab,tbs->tas", tiles, picked, preferred_element_type=jnp.float32)
    outgoing = (
        jnp.zeros((peer_count, tile_rows, slice_count), jnp.float32)
        .at[jnp.where(alive, tile_dest, peer_count)]
        .add(products, mode="drop")
    )
    incoming = lax.all_to_all(
        outgoing.astype(jnp.bfloat16), "dom", split_axis=0, concat_axis=0, tiled=True
    ).astype(jnp.float32)
    sinogram = jnp.zeros(counts.shape, jnp.float32).at[slot_block[0]].add(incoming)
    measured = jnp.log(flux / counts.astype(jnp.float32))
    residual = (sinogram - measured).astype(jnp.bfloat16)
    returned = lax.all_to_all(residual[slot_block[0]], "dom", split_axis=0, concat_axis=0, tiled=True)
    back = jnp.einsum("tab,tas->tbs", tiles, returned[tile_dest], preferred_element_type=jnp.float32)
    gradient = (
        jnp.zeros(volume.shape, jnp.float32)
        .at[jnp.where(alive, tile_voxel, voxel_blocks)]
        .add(back, mode="drop")
    )
    return jnp.maximum(volume - step_size * gradient, 0.0), residual


def on_device(tiles, volume, *rest):
    n = lax.axis_size("dom")
    need = tiles.size * 2 + n * volume.shape[0] * tiles.shape[1] * tiles.shape[2] * 6
    if need > VMEM_BUDGET or n % 2 or tiles.shape[0] % GROUP:
        return general(tiles, volume, *rest)
    return fused(tiles, volume, *rest)


def solution(mesh):
    both = P(("slab", "dom"), None, None)
    in_specs = (P("dom", None, None), both, P("dom"), P("dom"), P("dom", None), P("dom"), both)
    return jax.shard_map(on_device, mesh=mesh, in_specs=in_specs, out_specs=(both, both), check_vma=False)
```
